256 devices in a mesh: frame: 32 (over x, z), head: 8 (over y, core).
Axes of the slice: x: 4, y: 4, z: 8, core: 2. Of those that a mesh axis runs over, the one named last changes fastest.
Arguments:
- queries: bfloat16 [64, 16, 32, 1792], P('frame', None, None, 'head'), may hold values from -6 to 6
- key_vectors: bfloat16 [64, 16, 32, 1792], P('frame', None, None, 'head'), may hold values from -6 to 6
- value_vectors: bfloat16 [64, 16, 32, 1792], P('frame', None, None, 'head'), may hold values from -8 to 8
- frame_index: int32 [64], P('frame'), may hold values from 0 to 127, as said below
- height_index: int32 [16], replicated, may hold values from 0 to 31, as said below
- width_index: int32 [32], replicated, may hold values from 0 to 63, as said below
- frame_block: int32 [64], P('frame'), may hold values from 0 to 20, never falling along the last dimension, each value on 1 to 6 neighbouring positions
- conv_weight: bfloat16 [3, 1792, 2240], P(None, 'head'), may hold values from -0.078125 to 0.078125
- conv_bias: float32 [2240], replicated, may hold values from -0.8 to 0.8
Outputs:
- mixed_frames: bfloat16 [16, 64, 32, 2240], P('head', 'frame')
The draws below stay inside these ranges and needn't reach their ends.
Inputs may be any that keep to these rules, and one draw needn't show every extreme that they name: `frame_index`: strictly increasing over the frames, first entry 0, last entry 127. `height_index`: strictly increasing over the rows, first entry 0, last entry 31. `width_index`: strictly increasing over the columns, first entry 0, last entry 63.
All inputs are finite; a program needn't handle non-finite values.
Results may differ from the reference program's by a relative error of at most 0.0043.
The reference program's roundings to bfloat16 on the way (of `attended`) count: a program that leaves them out, or rounds other values in their place, can miss the bound.
Values may be sent and summed in bfloat16 or wider, within the bound.
No kernel may reach another device: no remote copies, remote signals or barrier semaphores. Data moves between devices by JAX's collectives and lax.ppermute only.
A program may use at most 128 MiB of HBM per device.

```python
import math
import jax
import jax.numpy as jnp
import numpy as np
from jax import lax

HD = 112
HEADS_DEV = 2
CHANNELS = 1792
C_OUT = 2240
FRAMES = 64
HGT = 16
WID = 32
N_HEAD = 8


def rising_positions(key, salt, length):
    inner_key = jax.random.fold_in(key, salt)
    chosen = jax.random.permutation(inner_key, 2 * length - 2)[:length - 2] + 1
    middle = jnp.sort(chosen.astype(jnp.int32))
    first = jnp.zeros((1,), jnp.int32)
    last = jnp.full((1,), 2 * length - 1, jnp.int32)
    return jnp.concatenate([first, middle, last]).astype(jnp.int32)


def draw_frame_index(key, part):
    return rising_positions(key, 11, FRAMES)


def draw_height_index(key, part):
    return rising_positions(key, 12, HGT)


def draw_width_index(key, part):
    return rising_positions(key, 13, WID)


def draw_value_vectors(key, part):
    base_key = jax.random.fold_in(key, 21)
    common_key, slope_key, frame_key, noise_key = jax.random.split(base_key, 4)
    common = jax.random.normal(common_key, (CHANNELS,), jnp.float32)
    slope = jax.random.normal(slope_key, (CHANNELS,), jnp.float32)
    frame_part = jax.random.normal(frame_key, (FRAMES, 1, 1, CHANNELS), jnp.float32)
    ramp = (2.0 * jnp.arange(FRAMES, dtype=jnp.float32) / max(FRAMES - 1, 1) - 1.0).reshape(FRAMES, 1, 1, 1)
    noise = jax.random.normal(noise_key, (FRAMES, HGT, WID, CHANNELS), jnp.float32)
    mean_part = 0.7 * common + 0.7 * slope * ramp + 0.4 * frame_part
    return jnp.clip(mean_part + noise, -8.0, 8.0).astype(jnp.bfloat16)


def steps_of(own_key, extent, shards, least, largest):
    level, own = 1.0, jax.random.fold_in(own_key, 6)
    for dim, blocks in shards:
        steps = jnp.exp(jax.random.uniform(jax.random.fold_in(own, dim), (blocks,), jnp.float32, least / len(shards), largest / len(shards)))
        level = level * jnp.repeat(steps, extent[dim] // blocks).reshape([-1 if axis == dim else 1 for axis in range(len(extent))])
    return level


def split_up(number_of, total, limit, skew):
    portions = [(1 << 20) // math.isqrt(grade ** skew) + 1 for grade in range(2, number_of + 1)]
    surplus, holding = total - limit - (number_of - 1), [1] * (number_of - 1)
    while surplus > 0:
        candidates = [i for i in range(number_of - 1) if holding[i] < limit]
        whole, remaining = sum([portions[i] for i in candidates]), surplus
        for i in candidates:
            extra = min(limit - holding[i], max(1, remaining * portions[i] // whole), surplus)
            holding[i] = holding[i] + extra
            surplus = surplus - extra
    return np.array([limit] + holding)


def ragged(key, count, total, bound, skew):
    if count == 2:
        one = jax.random.randint(key, (), max(1, total - bound), min(bound, total - 1) + 1)
        return jnp.stack([one, total - one])
    sizes = jnp.asarray(split_up(count, total, bound, skew), jnp.int32)
    couples = (count - 1) // 2
    giver, taker = sizes[1:1 + 2 * couples:2], sizes[2:2 + 2 * couples:2]
    margin = jnp.minimum(giver - 1, bound - taker)
    moved = jax.random.randint(jax.random.fold_in(key, 1), (couples,), 0, 1 << 20) % (margin + 1)
    sizes = sizes.at[1:1 + 2 * couples:2].set(giver - moved).at[2:2 + 2 * couples:2].set(taker + moved)
    return sizes[jax.random.permutation(jax.random.fold_in(key, 2), count)]


def centred(stream_key, shape, spread, limit, cuts=(), kind=jnp.bfloat16):
    factor_of = steps_of(stream_key, shape, cuts, -0.22, 0.18) if cuts else 1.0
    result = jax.random.normal(stream_key, shape, jnp.float32) * spread * factor_of
    return jnp.minimum(jnp.maximum(result, -limit), limit).astype(kind)


def setup_inputs(seed: int = 0) -> dict:
    key_of = jax.random.split(jax.random.key(seed), 10)
    queries = centred(key_of[0], (FRAMES, HGT, WID, CHANNELS), 1.0, 6.0, ((0, 32), (3, 8)))
    key_vectors = centred(key_of[1], (FRAMES, HGT, WID, CHANNELS), 1.0, 6.0, ((0, 32), (3, 8)))
    value_vectors = draw_value_vectors(jax.random.fold_in(key_of[9], 71), 0)
    frame_index = draw_frame_index(jax.random.fold_in(key_of[9], 71), 0)
    height_index = draw_height_index(jax.random.fold_in(key_of[9], 71), 0)
    width_index = draw_width_index(jax.random.fold_in(key_of[9], 71), 0)
    frame_block = jnp.searchsorted(jnp.cumsum(ragged(key_of[6], FRAMES // 3, FRAMES, 6, 1)), jnp.arange(FRAMES), side="right").astype(jnp.int32)
    conv_weight = centred(key_of[7], (3, CHANNELS, C_OUT), (3 * CHANNELS) ** -0.5, 0.078125, ((1, 8),))
    conv_bias = centred(key_of[8], (C_OUT,), 0.2, 0.8, (), jnp.float32)
    return {"queries": queries, "key_vectors": key_vectors, "value_vectors": value_vectors, "frame_index": frame_index, "height_index": height_index, "width_index": width_index, "frame_block": frame_block, "conv_weight": conv_weight, "conv_bias": conv_bias}


EPSILON = 1e-6
HIGHEST = lax.Precision.HIGHEST


def spin_part(section, positions, axis_slot):
    half_size = section.shape[-1] // 2
    inverse = 10000.0 ** (-2.0 * jnp.arange(half_size, dtype=jnp.float32) / section.shape[-1])
    angles = positions.astype(jnp.float32)[:, None] * inverse[None, :]
    target = [1, 1, 1, 1, half_size]
    target[axis_slot] = positions.shape[0]
    angles = angles.reshape(target)
    cosine = jnp.cos(angles)
    sine_values = jnp.sin(angles)
    lower_half = section[..., :half_size]
    upper_half = section[..., half_size:]
    return jnp.concatenate([lower_half * cosine - upper_half * sine_values, upper_half * cosine + lower_half * sine_values], axis=-1)


def rotate(values, frame_pos, height_pos, width_pos):
    head_size = values.shape[-1]
    side_size = (head_size * 5 // 14) // 2 * 2
    first_size = head_size - 2 * side_size
    return jnp.concatenate([
        spin_part(values[..., :first_size], frame_pos, 0),
        spin_part(values[..., first_size:first_size + side_size], height_pos, 1),
        spin_part(values[..., first_size + side_size:], width_pos, 2)], axis=-1)


def reference(queries, key_vectors, value_vectors, frame_index, height_index, width_index, frame_block, conv_weight, conv_bias):
    group_width = HEADS_DEV * HD
    split_shape = (FRAMES, HGT, WID, HEADS_DEV, HD)
    allowed = (frame_block[None, :] <= frame_block[:, None]).astype(jnp.float32)
    summed = jnp.zeros((FRAMES, HGT, WID, C_OUT), jnp.float32)
    for group_index in range(N_HEAD):
        columns = slice(group_index * group_width, (group_index + 1) * group_width)
        query_pos = jax.nn.relu(queries[..., columns].astype(jnp.float32)).reshape(split_shape)
        key_pos = jax.nn.relu(key_vectors[..., columns].astype(jnp.float32)).reshape(split_shape)
        value_rows = value_vectors[..., columns].astype(jnp.float32).reshape(split_shape)
        query_rot = rotate(query_pos, frame_index, height_index, width_index)
        key_rot = rotate(key_pos, frame_index, height_index, width_index)
        frame_states = jnp.einsum('fyxhd,fyxhe->fhde', key_rot, value_rows, precision=HIGHEST)
        frame_sums = jnp.sum(key_pos, axis=(1, 2))
        states = jnp.einsum('tf,fhde->thde', allowed, frame_states, precision=HIGHEST)
        key_totals = jnp.einsum('tf,fhd->thd', allowed, frame_sums, precision=HIGHEST)
        numerator = jnp.einsum('tyxhd,thde->tyxhe', query_rot, states, precision=HIGHEST)
        denominator = jnp.einsum('tyxhd,thd->tyxh', query_pos, key_totals, precision=HIGHEST) + EPSILON
        attended = (numerator / denominator[..., None]).astype(jnp.bfloat16).reshape(FRAMES, HGT, WID, group_width)
        padded = jnp.concatenate([jnp.zeros((2, HGT, WID, group_width), jnp.bfloat16), attended], axis=0)
        for tap_index in range(3):
            shifted = padded[2 - tap_index:2 - tap_index + FRAMES].reshape(-1, group_width)
            product = jnp.dot(shifted, conv_weight[tap_index, columns], preferred_element_type=jnp.float32)
            summed = summed + product.reshape(FRAMES, HGT, WID, C_OUT)
    activated = jax.nn.silu(summed + conv_bias).astype(jnp.bfloat16)
    return jnp.transpose(activated, (1, 0, 2, 3))
```

```python
import functools

import jax
import jax.numpy as jnp
import numpy as np
from jax import lax
from jax.experimental import pallas as pl
from jax.experimental.pallas import tpu as pltpu
from jax.sharding import PartitionSpec as P

HD = 112
LANES = 2 * HD
SIDE = HD * 5 // 14 // 2 * 2
ROWS = 120
EPSILON = 1e-06
BF = jnp.bfloat16
F32 = jnp.float32


def lane_tables():
    first = HD - 2 * SIDE
    freq = np.zeros(LANES, np.float64)
    section = np.zeros(LANES, np.int32)
    pairing = np.zeros((LANES, LANES), np.float32)
    for head in range(2):
        start = head * HD
        for number, size in enumerate((first, SIDE, SIDE)):
            half = size // 2
            for j in range(half):
                low, high = start + j, start + j + half
                freq[low] = freq[high] = 10000.0 ** (-2.0 * j / size)
                section[low] = section[high] = number
                pairing[high, low] = -1.0
                pairing[low, high] = 1.0
            start += size
    same_head = (np.arange(LANES)[:, None] // HD == np.arange(LANES)[None, :] // HD).astype(np.float32)
    return freq.astype(np.float32), section, pairing, same_head


FREQ, SECTION, PAIRING, SAME_HEAD = lane_tables()


def split_hi_lo(value):
    hi = value.astype(BF)
    return hi, (value - hi.astype(F32)).astype(BF)


def dot(a, b):
    return jnp.dot(a, b, preferred_element_type=F32)


def dot_t(a, b):
    return lax.dot_general(a, b, (((0,), (0,)), ((), ())), preferred_element_type=F32)


def rotated(positive, time_cos, time_sin, side_cos, side_sin, pairing):
    height, width, lanes = positive.shape
    flat = positive.reshape(height * width, lanes)
    partner = dot(flat, pairing)
    cos = (side_cos[:height] + time_cos)[:, None, :] + side_cos[height:][None, :, :]
    sin = (side_sin[:height] + time_sin)[:, None, :] + side_sin[height:][None, :, :]
    wide = flat.astype(F32)
    return wide, wide * cos.reshape(height * width, lanes) + partner * sin.reshape(height * width, lanes)


def state_kernel(ids, k_ref, v_ref, tc_ref, ts_ref, sc_ref, ss_ref, pair_ref, out_ref):
    g = pl.program_id(0)
    key = jnp.maximum(k_ref[0], 0)
    wide, rot = rotated(key, tc_ref[pl.ds(g, 1)], ts_ref[pl.ds(g, 1)], sc_ref[...], ss_ref[...], pair_ref[...])
    value = v_ref[0].reshape(wide.shape)
    hi, lo = split_hi_lo(rot)
    outer = dot_t(hi, value) + dot_t(lo, value)
    lane = lax.broadcasted_iota(jnp.int32, (HD, LANES), 1)
    out_ref[0, :HD] = jnp.where(lane < HD, outer[:HD], outer[HD:])
    row = lax.broadcasted_iota(jnp.int32, (ROWS - HD, LANES), 0)
    total = jnp.broadcast_to(jnp.sum(wide, axis=0, keepdims=True), row.shape)
    block = ids[g].astype(F32)
    position = ids[2 + g].astype(F32)
    out_ref[0, HD:] = jnp.where(row == 0, total, jnp.where(row == 1, block, jnp.where(row == 2, position, 0.0)))


def attend_kernel(q_ref, halo_ref, st_ref, tc_ref, ts_ref, sc_ref, ss_ref, pair_ref, same_ref, out_ref):
    e = pl.program_id(0)
    query = jnp.maximum(jnp.where(e < 2, halo_ref[0], q_ref[0]), 0)
    height, width, lanes = query.shape
    wide, rot = rotated(query, tc_ref[pl.ds(e, 1)], ts_ref[pl.ds(e, 1)], sc_ref[...], ss_ref[...], pair_ref[...])
    packed = st_ref[0, :HD]
    lane = lax.broadcasted_iota(jnp.int32, (HD, LANES), 1)
    full = jnp.concatenate([jnp.where(lane < HD, packed, 0.0), jnp.where(lane < HD, 0.0, packed)], axis=0)
    state_hi, state_lo = split_hi_lo(full)
    rot_hi, rot_lo = split_hi_lo(rot)
    numerator = dot(rot_hi, state_hi) + dot(rot_lo, state_hi) + dot(rot_hi, state_lo)
    w_hi, w_lo = split_hi_lo(wide * st_ref[0, HD : HD + 1])
    denominator = dot(w_hi, same_ref[...]) + dot(w_lo, same_ref[...]) + EPSILON
    out_ref[...] = (numerator / denominator).astype(BF).reshape(height, 1, width, lanes)


def conv_kernel(count, idx, *refs):
    blocks = refs[: 2 * count]
    w_ref, send_ref, keep_ref = refs[2 * count :]
    rows = None
    for tap in range(3):
        lhs = jnp.concatenate([b[:, 2 - tap : 4 - tap].reshape(-1, LANES) for b in blocks], axis=0)
        part = dot(lhs, w_ref[tap])
        rows = part if rows is None else rows + part
    each = rows.shape[0] // (2 * count)
    shape = send_ref.shape[1:]
    for j in range(count):
        send_ref[j] = rows[2 * j * each : (2 * j + 1) * each].astype(BF).reshape(shape)
        keep_ref[j] = rows[(2 * j + 1) * each : (2 * j + 2) * each].reshape(shape)


def whole(shape):
    return pl.BlockSpec(shape, lambda *_: (0,) * len(shape))


def conv_group(extended, weight, index, count):
    _, frames, width, lanes = extended.shape
    c_out = weight.shape[-1]
    tile = 768
    steps = pl.cdiv(c_out, tile)

    def row_block(slot):
        return pl.BlockSpec((2, frames, width, lanes), lambda n, idx: (idx[slot], 0, 0, 0))

    out_block = pl.BlockSpec((count, 2, 2, width, tile), lambda n, idx: (0, 0, 0, 0, n))
    shape = (count, 2, 2, width, c_out)
    return pl.pallas_call(
        functools.partial(conv_kernel, count),
        grid_spec=pltpu.PrefetchScalarGridSpec(
            num_scalar_prefetch=1,
            grid=(steps,),
            in_specs=[row_block(s) for s in range(2 * count)]
            + [pl.BlockSpec((3, lanes, tile), lambda n, idx: (0, 0, n))],
            out_specs=[out_block, out_block],
        ),
        out_shape=[jax.ShapeDtypeStruct(shape, BF), jax.ShapeDtypeStruct(shape, F32)],
        name="conv",
    )(index, *([extended] * (2 * count)), weight)


def shifted(value, by):
    length = lax.axis_size("frame")
    return lax.ppermute(value, "frame", [(i, i + by) for i in range(length) if 0 <= i + by < length])


def moved(value, dy, dc):
    chips = lax.axis_size("head") // 2
    return lax.ppermute(
        value, "head", [(y * 2 + c, (y + dy) % chips * 2 + (c + dc) % 2) for y in range(chips) for c in range(2)]
    )


def angle_tables(positions, section):
    angles = positions.astype(F32)[:, None] * FREQ[None, :]
    mine = (SECTION == section)[None, :]
    return jnp.where(mine, jnp.cos(angles), 0.0), jnp.where(mine, jnp.sin(angles), 0.0)


def per_device(
    queries, key_vectors, value_vectors, frame_index, height_index, width_index, frame_block, conv_weight, conv_bias
):
    frames, height, width, lanes = queries.shape
    pairing = jnp.asarray(PAIRING, BF)
    same_head = jnp.asarray(SAME_HEAD, BF)
    time_cos, time_sin = angle_tables(frame_index, 0)
    row_cos, row_sin = angle_tables(height_index, 1)
    col_cos, col_sin = angle_tables(width_index, 2)
    side_cos = jnp.concatenate([row_cos, col_cos], axis=0)
    side_sin = jnp.concatenate([row_sin, col_sin], axis=0)
    frame_spec = pl.BlockSpec((1, height, width, lanes), lambda g, ids: (g, 0, 0, 0))
    packed = pl.pallas_call(
        state_kernel,
        grid_spec=pltpu.PrefetchScalarGridSpec(
            num_scalar_prefetch=1,
            grid=(frames,),
            in_specs=[frame_spec, frame_spec]
            + [whole((frames, lanes))] * 2
            + [whole((height + width, lanes))] * 2
            + [whole((lanes, lanes))],
            out_specs=pl.BlockSpec((1, ROWS, lanes), lambda g, ids: (g, 0, 0)),
        ),
        out_shape=jax.ShapeDtypeStruct((frames, ROWS, lanes), F32),
        name="frame_state",
    )(
        jnp.concatenate([frame_block, frame_index]),
        key_vectors, value_vectors, time_cos, time_sin, side_cos, side_sin, pairing,
    )
    first, second = packed[0], packed[1]
    is_id = lax.broadcasted_iota(jnp.int32, first.shape, 0) == HD + 1
    ids = frame_block.astype(F32)
    joined = ids[0] == ids[1]

    before = shifted(packed, 1)
    halo = shifted(queries, 1)
    previous = before[0] + before[1]
    running = first + second + previous
    earlier = jnp.zeros_like(first)
    length = lax.axis_size("frame")
    by = 2
    while by < length:
        arrived = shifted(running, by)
        earlier = earlier + arrived
        running = running + arrived
        by *= 2
    lead = jnp.where(is_id, first, first + jnp.where(joined, second, 0.0))
    next_lead = shifted(lead, -1)
    next_id = next_lead[HD + 1, 0]
    pair_lead = jnp.where(is_id, lead, lead + jnp.where(joined & (next_id == ids[0]), next_lead, 0.0))
    far_lead = shifted(pair_lead, -2)
    tail = jnp.where(next_id == ids[1], next_lead, 0.0) + jnp.where(far_lead[HD + 1, 0] == ids[1], far_lead, 0.0)

    upto = earlier + previous
    state_1 = upto + first + second + tail
    state_0 = jnp.where(joined, state_1, upto + first)
    id_a, id_b = before[0, HD + 1, 0], before[1, HD + 1, 0]
    state_b = jnp.where(id_b == ids[0], state_0, upto)
    state_a = jnp.where(id_a == id_b, state_b, earlier + before[0])
    states = jnp.stack([state_a, state_b, state_0, state_1])

    halo_cos, halo_sin = angle_tables(before[:, HD + 2, 0], 0)
    all_cos = jnp.concatenate([halo_cos, time_cos], axis=0)
    all_sin = jnp.concatenate([halo_sin, time_sin], axis=0)
    extended = pl.pallas_call(
        attend_kernel,
        grid=(2 * frames,),
        in_specs=[
            pl.BlockSpec((1, height, width, lanes), lambda e: (jnp.maximum(e - 2, 0), 0, 0, 0)),
            pl.BlockSpec((1, height, width, lanes), lambda e: (jnp.minimum(e, 1), 0, 0, 0)),
            pl.BlockSpec((1, ROWS, lanes), lambda e: (e, 0, 0)),
            whole((2 * frames, lanes)), whole((2 * frames, lanes)),
            whole((height + width, lanes)), whole((height + width, lanes)),
            whole((lanes, lanes)), whole((lanes, lanes)),
        ],
        out_specs=pl.BlockSpec((height, 1, width, lanes), lambda e: (0, e, 0, 0)),
        out_shape=jax.ShapeDtypeStruct((height, 2 * frames, width, lanes), BF),
        name="attend",
    )(queries, halo, states, all_cos, all_sin, side_cos, side_sin, pairing, same_head)

    head = lax.axis_index("head")
    chips = lax.axis_size("head") // 2
    chip, core = head // 2, head % 2

    def slots(relatives):
        return jnp.stack([(chip + j) % chips * 2 + c for j in relatives for c in (1 - core, core)]).astype(jnp.int32)

    def chip_sums(relatives):
        send, keep = conv_group(extended, conv_weight, slots(relatives), len(relatives))
        return keep + moved(send, 0, 1).astype(F32)

    far = chip_sums((2,))
    from_far = moved(far[0].astype(BF), 2, 0)
    near = chip_sums((1, 3))
    from_low = moved(near[0].astype(BF), 1, 0)
    from_high = moved(near[1].astype(BF), 3, 0)
    own = chip_sums((0,))
    summed = own[0] + from_far.astype(F32) + from_low.astype(F32) + from_high.astype(F32)
    return jax.nn.silu(summed + conv_bias).astype(BF)


def solution(mesh):
    placed = (
        P("frame", None, None, "head"),
        P("frame", None, None, "head"),
        P("frame", None, None, "head"),
        P("frame"),
        P(),
        P(),
        P("frame"),
        P(None, "head", None),
        P(),
    )
    return jax.shard_map(
        per_device,
        mesh=mesh,
        in_specs=placed,
        out_specs=P("head", "frame", None, None),
        check_vma=False,
    )
```

```python
import functools

import jax
import jax.numpy as jnp
import numpy as np
from jax import lax
from jax.experimental import pallas as pl
from jax.experimental.pallas import tpu as pltpu
from jax.sharding import PartitionSpec as P


HD = 112
LANES = 2 * HD
SIDE = HD * 5 // 14 // 2 * 2
ROWS = 120
EPSILON = 1e-06
BF = jnp.bfloat16
F32 = jnp.float32


def lane_tables():
    first = HD - 2 * SIDE
    freq = np.zeros(LANES, np.float64)
    section = np.zeros(LANES, np.int32)
    pairing = np.zeros((LANES, LANES), np.float32)
    for head in range(2):
        start = head * HD
        for number, size in enumerate((first, SIDE, SIDE)):
            half = size // 2
            for j in range(half):
                low, high = start + j, start + j + half
                freq[low] = freq[high] = 10000.0 ** (-2.0 * j / size)
                section[low] = section[high] = number
                pairing[high, low] = -1.0
                pairing[low, high] = 1.0
            start += size
    same_head = (np.arange(LANES)[:, None] // HD == np.arange(LANES)[None, :] // HD).astype(np.float32)
    return freq.astype(np.float32), section, pairing, same_head


FREQ, _, PAIRING, SAME_HEAD = lane_tables()


def split_hi_lo(value):
    hi = value.astype(BF)
    return hi, (value - hi.astype(F32)).astype(BF)


def dot(a, b):
    return jnp.dot(a, b, preferred_element_type=F32)


def dot_t(a, b):
    return lax.dot_general(a, b, (((0,), (0,)), ((), ())), preferred_element_type=F32)


def side_angles(heights, widths, freq, cos_ref, sin_ref):
    rows, cols = heights.shape[0], widths.shape[0]
    positions = [heights[i] for i in range(rows)] + [widths[i] for i in range(cols)]
    lane = lax.broadcasted_iota(jnp.int32, (rows + cols, LANES), 1)
    lane = jnp.where(lane < HD, lane, lane - HD)
    row = lax.broadcasted_iota(jnp.int32, lane.shape, 0)
    first = HD - 2 * SIDE
    section = (lane >= first).astype(jnp.int32) + (lane >= first + SIDE).astype(jnp.int32)
    mine = section == jnp.where(row < rows, 1, 2)
    for i, position in enumerate(positions):
        cos_ref[i : i + 1] = freq * position.astype(F32)
    angles = cos_ref[...]
    sin_ref[...] = jnp.where(mine, jnp.sin(angles), 0.0)
    cos_ref[...] = jnp.where(mine, jnp.cos(angles), 0.0)


def time_tables(angle):
    lane = lax.broadcasted_iota(jnp.int32, angle.shape, 1)
    mine = jnp.where(lane < HD, lane, lane - HD) < HD - 2 * SIDE
    return jnp.where(mine, jnp.cos(angle), 0.0), jnp.where(mine, jnp.sin(angle), 0.0)


def rotated(positive, angle, side_cos, side_sin, pairing, height):
    _, width, lanes = positive.shape
    flat = positive.reshape(height * width, lanes)
    partner = dot(flat, pairing)
    time_cos, time_sin = time_tables(angle)
    cos = (side_cos[:height] + time_cos)[:, None, :] + side_cos[height:][None, :, :]
    sin = (side_sin[:height] + time_sin)[:, None, :] + side_sin[height:][None, :, :]
    wide = flat.astype(F32)
    return wide, wide * cos.reshape(height * width, lanes) + partner * sin.reshape(height * width, lanes)


def state_kernel(
    blocks, frames, heights, widths, k_ref, v_ref, freq_ref, pair_ref,
    first_ref, second_ref, total_ref, lead_ref, cos_ref, sin_ref,
):
    g = pl.program_id(0)
    height = k_ref.shape[1]

    @pl.when(g == 0)
    def _():
        side_angles(heights, widths, freq_ref[...], cos_ref, sin_ref)

    key = jnp.maximum(k_ref[0], 0)
    angle = freq_ref[...] * frames[g].astype(F32)
    wide, rot = rotated(key, angle, cos_ref[...], sin_ref[...], pair_ref[...], height)
    value = v_ref[0].reshape(wide.shape)
    hi, lo = split_hi_lo(rot)
    outer = dot_t(hi, value) + dot_t(lo, value)
    lane = lax.broadcasted_iota(jnp.int32, (HD, LANES), 1)
    state = jnp.where(lane < HD, outer[:HD], outer[HD:])
    row = lax.broadcasted_iota(jnp.int32, (ROWS - HD, LANES), 0)
    total = jnp.broadcast_to(jnp.sum(wide, axis=0, keepdims=True), row.shape)
    joined = (blocks[0] == blocks[1]).astype(F32)
    marks = [blocks[g], frames[g], None, frames[1 - g]]
    extra = jnp.where(row == 0, total, 0.0)
    for i, mark in enumerate(marks):
        extra = jnp.where(row == i + 1, joined if mark is None else mark.astype(F32), extra)

    @pl.when(g == 0)
    def _():
        first_ref[:HD] = state
        first_ref[HD:] = extra

    @pl.when(g == 1)
    def _():
        second_ref[:HD] = state
        second_ref[HD:] = extra
        total_ref[:HD] = first_ref[:HD] + state
        total_ref[HD:] = first_ref[HD:] + extra
        lead_ref[:HD] = first_ref[:HD] + joined * state
        lead_ref[HD:] = first_ref[HD:] + jnp.where(row == 0, joined * extra, 0.0)


def query_kernel(q_ref, halo_ref, prev_ref, own_ref, freq_ref, cos_ref, sin_ref, pair_ref, qp_ref, hi_ref, lo_ref):
    e = pl.program_id(0)
    query = jnp.maximum(jnp.where(e < 2, halo_ref[0], q_ref[0]), 0)
    height, _, _ = query.shape
    here, other = HD + 2, HD + 4
    rows = [prev_ref[other : other + 1], prev_ref[here : here + 1], own_ref[other : other + 1], own_ref[here : here + 1]]
    position = jnp.where(e < 2, jnp.where(e == 0, rows[0], rows[1]), jnp.where(e == 2, rows[2], rows[3]))
    _, rot = rotated(query, freq_ref[...] * position, cos_ref[...], sin_ref[...], pair_ref[...], height)
    hi, lo = split_hi_lo(rot)
    qp_ref[...] = query.reshape(qp_ref.shape)
    hi_ref[...] = hi.reshape(hi_ref.shape)
    lo_ref[...] = lo.reshape(lo_ref.shape)


def finish_states(first, second, prev, upto, next_lead, far_lead, same_head, sh_ref, sl_ref, kh_ref, kl_ref):
    mark = slice(HD + 1, HD + 2)
    joint = slice(HD + 3, HD + 4)
    tail = jnp.where(next_lead[mark] == second[mark], next_lead, 0.0)
    tail = tail + jnp.where(far_lead[mark] == second[mark], far_lead, 0.0)
    state_1 = upto + first + second + tail
    state_0 = jnp.where(second[joint] > 0.5, state_1, upto + first)
    state_b = jnp.where(prev[mark] == first[mark], state_0, upto)
    state_a = jnp.where(prev[joint] > 0.5, state_b, upto - prev)
    lane = lax.broadcasted_iota(jnp.int32, (HD, LANES), 1)
    square = (LANES, LANES)
    eye = lax.broadcasted_iota(jnp.int32, square, 0) == lax.broadcasted_iota(jnp.int32, square, 1)
    for e, state in enumerate((state_a, state_b, state_0, state_1)):
        packed = state[:HD]
        full = jnp.concatenate([jnp.where(lane < HD, packed, 0.0), jnp.where(lane < HD, 0.0, packed)], axis=0)
        sh_ref[e], sl_ref[e] = split_hi_lo(full)
        d_hi, d_lo = split_hi_lo(jnp.where(eye, state[HD : HD + 1], 0.0))
        kh_ref[e], kl_ref[e] = split_hi_lo(dot(d_hi, same_head) + dot(d_lo, same_head))


def conv_kernel(count, idx, *refs):
    groups = [refs[i * 2 * count : (i + 1) * 2 * count] for i in range(3)]
    records = refs[6 * count : 6 * count + 6]
    same_ref, w_ref, send_ref, keep_ref, lhs_ref, sh_ref, sl_ref, kh_ref, kl_ref = refs[6 * count + 6 :]
    width = groups[0][0].shape[2]
    each = 2 * width
    half = 2 * count * each

    def rows(blocks, e):
        return jnp.concatenate([b[:, e].reshape(each, LANES) for b in blocks], axis=0)

    finish_states(*(r[...] for r in records), same_ref[...], sh_ref, sl_ref, kh_ref, kl_ref)
    for e in range(4):
        query, hi, lo = (rows(blocks, e) for blocks in groups)
        numerator = dot(hi, sh_ref[e]) + dot(lo, sh_ref[e]) + dot(hi, sl_ref[e])
        denominator = dot(query, kh_ref[e]) + dot(query, kl_ref[e]) + EPSILON
        lhs_ref[e * half : (e + 1) * half] = (numerator / denominator).astype(BF)
    c_out = w_ref.shape[-1]
    tile = 768
    for col in range(0, c_out, tile):
        cols = slice(col, min(col + tile, c_out))
        part = dot(lhs_ref[2 * half :], w_ref[0, :, cols])
        part = part + dot(lhs_ref[half : 3 * half], w_ref[1, :, cols])
        part = part + dot(lhs_ref[: 2 * half], w_ref[2, :, cols])
        for t in range(2):
            for s in range(2 * count):
                at = (t * 2 * count + s) * each
                piece = part[at : at + each].reshape(2, width, -1)
                if s % 2 == 0:
                    send_ref[s // 2, :, t, :, cols] = piece.astype(BF)
                else:
                    keep_ref[s // 2, :, t, :, cols] = piece


LIMIT = pltpu.CompilerParams(vmem_limit_bytes=24 << 20)


def off_chip(*values):
    return [pltpu.with_memory_space_constraint(v, pltpu.HBM) for v in values]


def whole(shape):
    return pl.BlockSpec(shape, lambda *_: (0,) * len(shape))


def conv_group(index, queries, records, same_head, weight, count):
    _, frames, width, lanes = queries[0].shape

    def row_block(slot):
        return pl.BlockSpec((2, frames, width, lanes), lambda n, idx: (idx[slot], 0, 0, 0))

    in_vmem = pl.BlockSpec(memory_space=pltpu.VMEM)
    shape = (count, 2, 2, width, weight.shape[-1])
    return pl.pallas_call(
        functools.partial(conv_kernel, count),
        grid_spec=pltpu.PrefetchScalarGridSpec(
            num_scalar_prefetch=1,
            grid=(1,),
            in_specs=[row_block(s) for _ in queries for s in range(2 * count)]
            + [whole((ROWS, lanes))] * 6
            + [whole((lanes, lanes)), in_vmem],
            out_specs=[whole(shape)] * 2,
            scratch_shapes=[pltpu.VMEM((frames * 2 * count * 2 * width, lanes), BF)]
            + [pltpu.VMEM((frames, lanes, lanes), BF)] * 4,
        ),
        out_shape=[pltpu.HBM(shape, BF), pltpu.HBM(shape, F32)],
        compiler_params=LIMIT,
        name="conv",
    )(index, *[q for q in queries for _ in range(2 * count)], *records, same_head, weight)


def shifted(value, by):
    length = lax.axis_size("frame")
    return lax.ppermute(value, "frame", [(i, i + by) for i in range(length) if 0 <= i + by < length])


def swapped(value, mask):
    return lax.ppermute(value, "frame", [(i, i ^ mask) for i in range(lax.axis_size("frame"))])


def moved(value, dy, dc):
    chips = lax.axis_size("head") // 2
    return lax.ppermute(
        value, "head", [(y * 2 + c, (y + dy) % chips * 2 + (c + dc) % 2) for y in range(chips) for c in range(2)]
    )


def block(
    queries, key_vectors, value_vectors, frame_index, height_index, width_index, frame_block, conv_weight, conv_bias
):
    frames, height, width, lanes = queries.shape
    pairing = jnp.asarray(PAIRING, BF)
    same_head = jnp.asarray(SAME_HEAD, BF)
    freq = jnp.asarray(FREQ)[None, :]
    frame_spec = pl.BlockSpec((1, height, width, lanes), lambda g, *_: (g, 0, 0, 0))
    record = (ROWS, lanes)
    table = (height + width, lanes)
    first, second, total, lead, side_cos, side_sin = pl.pallas_call(
        state_kernel,
        grid_spec=pltpu.PrefetchScalarGridSpec(
            num_scalar_prefetch=4,
            grid=(frames,),
            in_specs=[frame_spec, frame_spec, whole((1, lanes)), whole((lanes, lanes))],
            out_specs=[whole(record)] * 4 + [whole(table)] * 2,
        ),
        out_shape=[pltpu.HBM(record, F32)] * 2
        + [jax.ShapeDtypeStruct(record, F32)] * 2
        + [pltpu.HBM(table, F32)] * 2,
        compiler_params=LIMIT,
        name="frame_state",
    )(*off_chip(frame_block, frame_index, height_index, width_index, key_vectors, value_vectors, freq, pairing))

    device = lax.axis_index("frame")
    depth = 8
    upto = jnp.zeros_like(total)
    running = total
    mask = 1
    while mask < depth:
        arrived = swapped(running, mask)
        upto = upto + jnp.where(device & mask != 0, arrived, 0.0)
        running = running + arrived
        mask *= 2
    across = []
    while mask < lax.axis_size("frame"):
        across.append((mask, swapped(running, mask)))
        mask += depth

    halo = shifted(queries, 1)
    prev = shifted(second, 1)
    next_lead = shifted(lead, -1)
    sums = lax.broadcasted_iota(jnp.int32, (ROWS, 1), 0) <= HD
    mark = slice(HD + 1, HD + 2)
    chained = (next_lead[mark] == lead[mark]) & (lead[HD + 3 : HD + 4] > 0.5)
    pair_lead = lead + jnp.where(sums & chained, next_lead, 0.0)
    far_lead = shifted(pair_lead, -2)

    query_block = pl.BlockSpec((height, 1, width, lanes), lambda e: (0, e, 0, 0))
    query_shape = pltpu.HBM((height, 2 * frames, width, lanes), BF)
    query_call = pl.pallas_call(
        query_kernel,
        grid=(2 * frames,),
        in_specs=[
            pl.BlockSpec((1, height, width, lanes), lambda e: (jnp.maximum(e - 2, 0), 0, 0, 0)),
            pl.BlockSpec((1, height, width, lanes), lambda e: (jnp.minimum(e, 1), 0, 0, 0)),
            whole(record), whole(record), whole((1, lanes)), whole(table), whole(table), whole((lanes, lanes)),
        ],
        out_specs=[query_block] * 3,
        out_shape=[query_shape] * 3,
        compiler_params=LIMIT,
        name="queries",
    )
    positive, rot_hi, rot_lo = query_call(
        *off_chip(queries, halo, prev, second, freq, side_cos, side_sin, pairing)
    )

    positive, rot_hi, rot_lo, across = lax.optimization_barrier((positive, rot_hi, rot_lo, across))
    for mask, arrived in across:
        upto = upto + jnp.where(device ^ mask < device, arrived, 0.0)
    records = off_chip(first, second, prev, upto, next_lead, far_lead)

    head = lax.axis_index("head")
    chips = lax.axis_size("head") // 2
    chip, core = head // 2, head % 2
    weight = pltpu.with_memory_space_constraint(conv_weight, pltpu.VMEM)
    (same,) = off_chip(same_head)
    rotated_queries = off_chip(positive, rot_hi, rot_lo)

    def slots(*relatives):
        return jnp.stack([(chip + j) % chips * 2 + c for j in relatives for c in (1 - core, core)]).astype(jnp.int32)

    def conv(index):
        return conv_group(index, rotated_queries, records, same, weight, index.shape[0] // 2)

    send, keep = conv(slots(2))
    far = (keep[0] + moved(send[0], 0, 1).astype(F32)).astype(BF)
    from_far = moved(far, 2, 0)
    far, near_index = lax.optimization_barrier((far, slots(1, 3)))
    send, keep = conv(near_index)
    swap = moved(send, 0, 1)
    near = (keep + swap.astype(F32)).astype(BF)
    from_low = moved(near[0], 1, 0)
    from_high = moved(near[1], 3, 0)
    near, own_index = lax.optimization_barrier((near, slots(0)))
    own_send, own = conv(own_index)
    own = own[0] + moved(own_send[0], 0, 1).astype(F32)
    summed = own + from_far.astype(F32) + from_low.astype(F32) + from_high.astype(F32)
    return jax.nn.silu(summed + conv_bias).astype(BF)


def solution(mesh):
    placed = (
        P("frame", None, None, "head"),
        P("frame", None, None, "head"),
        P("frame", None, None, "head"),
        P("frame"),
        P(),
        P(),
        P("frame"),
        P(None, "head", None),
        P(),
    )
    return jax.shard_map(
        block,
        mesh=mesh,
        in_specs=placed,
        out_specs=P("head", "frame", None, None),
        check_vma=False,
    )
```

```python
import functools

import jax
import jax.numpy as jnp
import numpy as np
from jax import lax
from jax.experimental import pallas as pl
from jax.experimental.pallas import tpu as pltpu
from jax.sharding import PartitionSpec as P


HD = 112
LANES = 2 * HD
SIDE = HD * 5 // 14 // 2 * 2
ROWS = 120
EPSILON = 1e-06
BF = jnp.bfloat16
F32 = jnp.float32


def lane_tables():
    first = HD - 2 * SIDE
    freq = np.zeros(LANES, np.float64)
    section = np.zeros(LANES, np.int32)
    pairing = np.zeros((LANES, LANES), np.float32)
    for head in range(2):
        start = head * HD
        for number, size in enumerate((first, SIDE, SIDE)):
            half = size // 2
            for j in range(half):
                low, high = start + j, start + j + half
                freq[low] = freq[high] = 10000.0 ** (-2.0 * j / size)
                section[low] = section[high] = number
                pairing[high, low] = -1.0
                pairing[low, high] = 1.0
            start += size
    same_head = (np.arange(LANES)[:, None] // HD == np.arange(LANES)[None, :] // HD).astype(np.float32)
    return freq.astype(np.float32), section, pairing, same_head


FREQ, _, PAIRING, SAME_HEAD = lane_tables()


def split_hi_lo(value):
    hi = value.astype(BF)
    return hi, (value - hi.astype(F32)).astype(BF)


def dot(a, b):
    return jnp.dot(a, b, preferred_element_type=F32)


def dot_t(a, b):
    return lax.dot_general(a, b, (((0,), (0,)), ((), ())), preferred_element_type=F32)


def side_angles(heights, widths, freq, cos_ref, sin_ref):
    rows, cols = heights.shape[0], widths.shape[0]
    positions = [heights[i] for i in range(rows)] + [widths[i] for i in range(cols)]
    lane = lax.broadcasted_iota(jnp.int32, (rows + cols, LANES), 1)
    lane = jnp.where(lane < HD, lane, lane - HD)
    row = lax.broadcasted_iota(jnp.int32, lane.shape, 0)
    first = HD - 2 * SIDE
    section = (lane >= first).astype(jnp.int32) + (lane >= first + SIDE).astype(jnp.int32)
    mine = section == jnp.where(row < rows, 1, 2)
    for i, position in enumerate(positions):
        cos_ref[i : i + 1] = freq * position.astype(F32)
    angles = cos_ref[...]
    sin_ref[...] = jnp.where(mine, jnp.sin(angles), 0.0)
    cos_ref[...] = jnp.where(mine, jnp.cos(angles), 0.0)


def time_tables(angle):
    lane = lax.broadcasted_iota(jnp.int32, angle.shape, 1)
    mine = jnp.where(lane < HD, lane, lane - HD) < HD - 2 * SIDE
    return jnp.where(mine, jnp.cos(angle), 0.0), jnp.where(mine, jnp.sin(angle), 0.0)


def rotated(positive, angle, side_cos, side_sin, pairing, height):
    _, width, lanes = positive.shape
    flat = positive.reshape(height * width, lanes)
    partner = dot(flat, pairing)
    time_cos, time_sin = time_tables(angle)
    cos = (side_cos[:height] + time_cos)[:, None, :] + side_cos[height:][None, :, :]
    sin = (side_sin[:height] + time_sin)[:, None, :] + side_sin[height:][None, :, :]
    wide = flat.astype(F32)
    return wide, wide * cos.reshape(height * width, lanes) + partner * sin.reshape(height * width, lanes)


def state_kernel(
    blocks, frames, heights, widths, k_ref, v_ref, freq_ref, pair_ref,
    first_ref, second_ref, total_ref, lead_ref, cos_ref, sin_ref,
):
    g = pl.program_id(0)
    height = k_ref.shape[1]

    @pl.when(g == 0)
    def _():
        side_angles(heights, widths, freq_ref[...], cos_ref, sin_ref)

    key = jnp.maximum(k_ref[0], 0)
    angle = freq_ref[...] * frames[g].astype(F32)
    wide, rot = rotated(key, angle, cos_ref[...], sin_ref[...], pair_ref[...], height)
    value = v_ref[0].reshape(wide.shape)
    hi, lo = split_hi_lo(rot)
    outer = dot_t(hi, value) + dot_t(lo, value)
    lane = lax.broadcasted_iota(jnp.int32, (HD, LANES), 1)
    state = jnp.where(lane < HD, outer[:HD], outer[HD:])
    row = lax.broadcasted_iota(jnp.int32, (ROWS - HD, LANES), 0)
    total = jnp.broadcast_to(jnp.sum(wide, axis=0, keepdims=True), row.shape)
    joined = (blocks[0] == blocks[1]).astype(F32)
    marks = [blocks[g], frames[g], None, frames[1 - g]]
    extra = jnp.where(row == 0, total, 0.0)
    for i, mark in enumerate(marks):
        extra = jnp.where(row == i + 1, joined if mark is None else mark.astype(F32), extra)

    @pl.when(g == 0)
    def _():
        first_ref[:HD] = state
        first_ref[HD:] = extra

    @pl.when(g == 1)
    def _():
        second_ref[:HD] = state
        second_ref[HD:] = extra
        total_ref[:HD] = first_ref[:HD] + state
        total_ref[HD:] = first_ref[HD:] + extra
        lead_ref[:HD] = first_ref[:HD] + joined * state
        lead_ref[HD:] = first_ref[HD:] + jnp.where(row == 0, joined * extra, 0.0)


def query_kernel(q_ref, halo_ref, prev_ref, own_ref, freq_ref, cos_ref, sin_ref, pair_ref, qp_ref, hi_ref, lo_ref):
    e = pl.program_id(0)
    query = jnp.maximum(jnp.where(e < 2, halo_ref[0], q_ref[0]), 0)
    height, _, _ = query.shape
    here, other = HD + 2, HD + 4
    rows = [prev_ref[other : other + 1], prev_ref[here : here + 1], own_ref[other : other + 1], own_ref[here : here + 1]]
    position = jnp.where(e < 2, jnp.where(e == 0, rows[0], rows[1]), jnp.where(e == 2, rows[2], rows[3]))
    _, rot = rotated(query, freq_ref[...] * position, cos_ref[...], sin_ref[...], pair_ref[...], height)
    hi, lo = split_hi_lo(rot)
    qp_ref[...] = query.reshape(qp_ref.shape)
    hi_ref[...] = hi.reshape(hi_ref.shape)
    lo_ref[...] = lo.reshape(lo_ref.shape)


def finish_states(first, second, prev, upto, next_lead, far_lead, same_head, sh_ref, sl_ref, kh_ref, kl_ref):
    mark = slice(HD + 1, HD + 2)
    joint = slice(HD + 3, HD + 4)
    tail = jnp.where(next_lead[mark] == second[mark], next_lead, 0.0)
    tail = tail + jnp.where(far_lead[mark] == second[mark], far_lead, 0.0)
    state_1 = upto + first + second + tail
    state_0 = jnp.where(second[joint] > 0.5, state_1, upto + first)
    state_b = jnp.where(prev[mark] == first[mark], state_0, upto)
    state_a = jnp.where(prev[joint] > 0.5, state_b, upto - prev)
    lane = lax.broadcasted_iota(jnp.int32, (HD, LANES), 1)
    square = (LANES, LANES)
    eye = lax.broadcasted_iota(jnp.int32, square, 0) == lax.broadcasted_iota(jnp.int32, square, 1)
    for e, state in enumerate((state_a, state_b, state_0, state_1)):
        packed = state[:HD]
        full = jnp.concatenate([jnp.where(lane < HD, packed, 0.0), jnp.where(lane < HD, 0.0, packed)], axis=0)
        sh_ref[e], sl_ref[e] = split_hi_lo(full)
        d_hi, d_lo = split_hi_lo(jnp.where(eye, state[HD : HD + 1], 0.0))
        kh_ref[e], kl_ref[e] = split_hi_lo(dot(d_hi, same_head) + dot(d_lo, same_head))


def attend_kernel(
    flags, qp_ref, hi_ref, lo_ref, first_ref, second_ref, prev_ref, next_ref, far_ref, upto_ref, a_ref, b_ref, c_ref,
    same_ref, mine_ref, other_ref, rows_ref, sh_ref, sl_ref, kh_ref, kl_ref,
):
    height, frames, width, lanes = qp_ref.shape
    upto = upto_ref[...]
    for i, arrived in enumerate((a_ref, b_ref, c_ref)):
        upto = upto + jnp.where(flags[i + 1] != 0, arrived[...], 0.0)
    records = (first_ref[...], second_ref[...], prev_ref[...], upto, next_ref[...], far_ref[...])
    finish_states(*records, same_ref[...], sh_ref, sl_ref, kh_ref, kl_ref)
    mine = flags[0]
    for e in range(frames):
        query, hi, lo = (r[:, e].reshape(height * width, lanes) for r in (qp_ref, hi_ref, lo_ref))
        numerator = dot(hi, sh_ref[e]) + dot(lo, sh_ref[e]) + dot(hi, sl_ref[e])
        denominator = dot(query, kh_ref[e]) + dot(query, kl_ref[e]) + EPSILON
        rows_ref[...] = (numerator / denominator).astype(BF).reshape(height, width, lanes)
        for chip in range(height // 4):
            out = slice(2 * chip, 2 * chip + 2)
            mine_ref[out, e] = rows_ref[pl.ds(4 * chip + 2 * mine, 2)]
            other_ref[out, e] = rows_ref[pl.ds(4 * chip + 2 - 2 * mine, 2)]


def conv_kernel(count, idx, *refs):
    parts = (refs[:count], refs[count : 2 * count])
    weights = refs[2 * count : 2 * count + 2]
    outs = refs[2 * count + 2 :]
    width = parts[0][0].shape[2]
    each = 2 * width
    lhs = [
        [
            jnp.concatenate([b[:, 2 - tap + t].reshape(each, LANES) for b in blocks for t in range(2)], axis=0)
            for tap in range(3)
        ]
        for blocks in parts
    ]

    def columns(col, size):
        total = None
        for blocks, w_ref in zip(lhs, weights):
            for tap in range(3):
                part = dot(blocks[tap], w_ref[tap, :, col : col + size])
                total = part if total is None else total + part
        for j in range(count):
            for t in range(2):
                at = (2 * j + t) * each
                outs[j][:, t, :, :size] = total[at : at + each].reshape(2, width, size).astype(outs[j].dtype)

    c_out = weights[0].shape[-1]
    for number, col in enumerate(range(0, c_out, TILE)):
        pl.when(pl.program_id(0) == number)(functools.partial(columns, col, min(TILE, c_out - col)))


TILE = 768
LIMIT = pltpu.CompilerParams(vmem_limit_bytes=24 << 20)


def off_chip(*values):
    return [pltpu.with_memory_space_constraint(v, pltpu.HBM) for v in values]


def whole(shape):
    return pl.BlockSpec(shape, lambda *_: (0,) * len(shape))


def attend(flags, queries, records, same_head):
    height, frames, width, lanes = queries[0].shape
    half = (height // 2, frames, width, lanes)
    square = pltpu.VMEM((frames, lanes, lanes), BF)
    in_vmem = pl.BlockSpec(memory_space=pltpu.VMEM)
    return pl.pallas_call(
        attend_kernel,
        grid_spec=pltpu.PrefetchScalarGridSpec(
            num_scalar_prefetch=1,
            grid=(1,),
            in_specs=[in_vmem] * 3 + [whole((ROWS, lanes))] * 9 + [whole((lanes, lanes))],
            out_specs=[in_vmem] * 2,
            scratch_shapes=[pltpu.VMEM((height, width, lanes), BF)] + [square] * 4,
        ),
        out_shape=[pltpu.VMEM(half, BF)] * 2,
        compiler_params=LIMIT,
        name="attend",
    )(flags, *queries, *records, same_head)


def conv_group(index, slots, attended, weights, dtype):
    _, frames, width, lanes = attended[0].shape
    count = len(slots)
    c_out = weights[0].shape[-1]

    def row_block(slot):
        return pl.BlockSpec((2, frames, width, lanes), lambda n, idx: (idx[slot], 0, 0, 0))

    return pl.pallas_call(
        functools.partial(conv_kernel, count),
        grid_spec=pltpu.PrefetchScalarGridSpec(
            num_scalar_prefetch=1,
            grid=(pl.cdiv(c_out, TILE),),
            in_specs=[row_block(s) for _ in attended for s in slots] + [pl.BlockSpec(memory_space=pltpu.VMEM)] * 2,
            out_specs=[pl.BlockSpec((2, 2, width, TILE), lambda n, idx: (0, 0, 0, n))] * count,
        ),
        out_shape=[pltpu.HBM((2, 2, width, c_out), dtype)] * count,
        compiler_params=LIMIT,
        name="conv",
    )(index, *[a for a in attended for _ in slots], *weights)


def shifted(value, by):
    length = lax.axis_size("frame")
    return lax.ppermute(value, "frame", [(i, i + by) for i in range(length) if 0 <= i + by < length])


def swapped(value, mask):
    return lax.ppermute(value, "frame", [(i, i ^ mask) for i in range(lax.axis_size("frame"))])


def moved(value, dy, dc):
    chips = lax.axis_size("head") // 2
    return lax.ppermute(
        value, "head", [(y * 2 + c, (y + dy) % chips * 2 + (c + dc) % 2) for y in range(chips) for c in range(2)]
    )


def block(
    queries, key_vectors, value_vectors, frame_index, height_index, width_index, frame_block, conv_weight, conv_bias
):
    frames, height, width, lanes = queries.shape
    pairing = jnp.asarray(PAIRING, BF)
    same_head = jnp.asarray(SAME_HEAD, BF)
    freq = jnp.asarray(FREQ)[None, :]
    frame_spec = pl.BlockSpec((1, height, width, lanes), lambda g, *_: (g, 0, 0, 0))
    record = (ROWS, lanes)
    table = (height + width, lanes)
    state_call = pl.pallas_call(
        state_kernel,
        grid_spec=pltpu.PrefetchScalarGridSpec(
            num_scalar_prefetch=4,
            grid=(frames,),
            in_specs=[frame_spec, frame_spec, whole((1, lanes)), whole((lanes, lanes))],
            out_specs=[whole(record)] * 4 + [whole(table)] * 2,
        ),
        out_shape=[pltpu.HBM(record, F32)] * 2
        + [jax.ShapeDtypeStruct(record, F32)] * 2
        + [pltpu.HBM(table, F32)] * 2,
        compiler_params=LIMIT,
        name="frame_state",
    )
    first, second, total, lead, side_cos, side_sin = state_call(*off_chip(frame_block, frame_index, height_index, width_index, key_vectors, value_vectors, freq, pairing))

    device = lax.axis_index("frame")
    depth = 8
    upto = jnp.zeros_like(total)
    running = total
    mask = 1
    while mask < depth:
        arrived = swapped(running, depth - 1 if 2 * mask == depth else mask)
        upto = upto + jnp.where(device & mask != 0, arrived, 0.0)
        running = running + arrived
        mask *= 2
    across = []
    while mask < lax.axis_size("frame"):
        across.append(swapped(running, mask))
        mask += depth

    their_weight = moved(conv_weight, 0, 1)
    halo = shifted(queries, 1)
    prev = shifted(second, 1)
    next_lead = shifted(lead, -1)
    sums = lax.broadcasted_iota(jnp.int32, (ROWS, 1), 0) <= HD
    mark = slice(HD + 1, HD + 2)
    chained = (next_lead[mark] == lead[mark]) & (lead[HD + 3 : HD + 4] > 0.5)
    pair_lead = lead + jnp.where(sums & chained, next_lead, 0.0)
    far_lead = shifted(pair_lead, -2)

    query_block = pl.BlockSpec((height, 1, width, lanes), lambda e: (0, e, 0, 0))
    query_shape = pltpu.VMEM((height, 2 * frames, width, lanes), BF)
    query_call = pl.pallas_call(
        query_kernel,
        grid=(2 * frames,),
        in_specs=[
            pl.BlockSpec((1, height, width, lanes), lambda e: (jnp.maximum(e - 2, 0), 0, 0, 0)),
            pl.BlockSpec((1, height, width, lanes), lambda e: (jnp.minimum(e, 1), 0, 0, 0)),
            whole(record), whole(record), whole((1, lanes)), whole(table), whole(table), whole((lanes, lanes)),
        ],
        out_specs=[query_block] * 3,
        out_shape=[query_shape] * 3,
        compiler_params=LIMIT,
        name="queries",
    )
    positive, rot_hi, rot_lo = query_call(
        *off_chip(queries, halo, prev, second, freq, side_cos, side_sin, pairing)
    )

    positive, rot_hi, rot_lo, across = lax.optimization_barrier((positive, rot_hi, rot_lo, across))
    records = (*off_chip(first, second, prev), next_lead, far_lead, upto, *across)

    head = lax.axis_index("head")
    chips = lax.axis_size("head") // 2
    chip, core = head // 2, head % 2
    (same,) = off_chip(same_head)
    owners = [(chip + j) % chips for j in (2, 1, 3, 0)]
    flags = jnp.stack([core] + [(device ^ m < device).astype(jnp.int32) for m in (8, 16, 24)] + owners).astype(jnp.int32)
    mine, other = attend(flags, (positive, rot_hi, rot_lo), records, same)
    theirs = moved(other, 0, 1)
    attended = (mine, theirs)
    weights = [pltpu.with_memory_space_constraint(w, pltpu.VMEM) for w in (conv_weight, their_weight)]
    (far,) = conv_group(flags, (4,), attended, weights, BF)
    from_far = moved(far, 2, 0)
    near = conv_group(flags, (5, 6), attended, weights, BF)
    from_low = moved(near[0], 1, 0)
    from_high = moved(near[1], 3, 0)
    (own,) = conv_group(flags, (7,), attended, weights, F32)
    own = own + from_far.astype(F32)
    summed = lax.optimization_barrier(own) + from_low.astype(F32) + from_high.astype(F32)
    return jax.nn.silu(summed + conv_bias).astype(BF)


def solution(mesh):
    placed = (
        P("frame", None, None, "head"),
        P("frame", None, None, "head"),
        P("frame", None, None, "head"),
        P("frame"),
        P(),
        P(),
        P("frame"),
        P(None, "head", None),
        P(),
    )
    return jax.shard_map(
        block,
        mesh=mesh,
        in_specs=placed,
        out_specs=P("head", "frame", None, None),
        check_vma=False,
    )
```

```python
import functools

import jax
import jax.numpy as jnp
import numpy as np
from jax import lax
from jax.experimental import pallas as pl
from jax.experimental.pallas import tpu as pltpu
from jax.sharding import PartitionSpec as P


HD = 112
LANES = 2 * HD
SIDE = HD * 5 // 14 // 2 * 2
ROWS = 120
EPSILON = 1e-06
BF = jnp.bfloat16
F32 = jnp.float32


def lane_tables():
    first = HD - 2 * SIDE
    freq = np.zeros(LANES, np.float64)
    section = np.zeros(LANES, np.int32)
    pairing = np.zeros((LANES, LANES), np.float32)
    for head in range(2):
        start = head * HD
        for number, size in enumerate((first, SIDE, SIDE)):
            half = size // 2
            for j in range(half):
                low, high = start + j, start + j + half
                freq[low] = freq[high] = 10000.0 ** (-2.0 * j / size)
                section[low] = section[high] = number
                pairing[high, low] = -1.0
                pairing[low, high] = 1.0
            start += size
    same_head = (np.arange(LANES)[:, None] // HD == np.arange(LANES)[None, :] // HD).astype(np.float32)
    return freq.astype(np.float32), section, pairing, same_head


FREQ, _, PAIRING, SAME_HEAD = lane_tables()


def split_hi_lo(value):
    hi = value.astype(BF)
    return hi, (value - hi.astype(F32)).astype(BF)


def dot(a, b):
    return jnp.dot(a, b, preferred_element_type=F32)


def dot_t(a, b):
    return lax.dot_general(a, b, (((0,), (0,)), ((), ())), preferred_element_type=F32)


def side_angles(heights, widths, freq, cos_ref, sin_ref):
    rows, cols = heights.shape[0], widths.shape[0]
    positions = [heights[i] for i in range(rows)] + [widths[i] for i in range(cols)]
    lane = lax.broadcasted_iota(jnp.int32, (rows + cols, LANES), 1)
    lane = jnp.where(lane < HD, lane, lane - HD)
    row = lax.broadcasted_iota(jnp.int32, lane.shape, 0)
    first = HD - 2 * SIDE
    section = (lane >= first).astype(jnp.int32) + (lane >= first + SIDE).astype(jnp.int32)
    mine = section == jnp.where(row < rows, 1, 2)
    for i, position in enumerate(positions):
        cos_ref[i : i + 1] = freq * position.astype(F32)
    angles = cos_ref[...]
    sin_ref[...] = jnp.where(mine, jnp.sin(angles), 0.0)
    cos_ref[...] = jnp.where(mine, jnp.cos(angles), 0.0)


def time_tables(angle):
    lane = lax.broadcasted_iota(jnp.int32, angle.shape, 1)
    mine = jnp.where(lane < HD, lane, lane - HD) < HD - 2 * SIDE
    return jnp.where(mine, jnp.cos(angle), 0.0), jnp.where(mine, jnp.sin(angle), 0.0)


def rotated(positive, angle, side_cos, side_sin, pairing, height):
    _, width, lanes = positive.shape
    flat = positive.reshape(height * width, lanes)
    partner = dot(flat, pairing)
    time_cos, time_sin = time_tables(angle)
    cos = (side_cos[:height] + time_cos)[:, None, :] + side_cos[height:][None, :, :]
    sin = (side_sin[:height] + time_sin)[:, None, :] + side_sin[height:][None, :, :]
    wide = flat.astype(F32)
    return wide, wide * cos.reshape(height * width, lanes) + partner * sin.reshape(height * width, lanes)


def state_kernel(
    blocks, frames, heights, widths, k_ref, v_ref, freq_ref, pair_ref,
    first_ref, second_ref, total_ref, lead_ref, cos_ref, sin_ref,
):
    g = pl.program_id(0)
    height = k_ref.shape[1]

    @pl.when(g == 0)
    def _():
        side_angles(heights, widths, freq_ref[...], cos_ref, sin_ref)

    key = jnp.maximum(k_ref[0], 0)
    angle = freq_ref[...] * frames[g].astype(F32)
    wide, rot = rotated(key, angle, cos_ref[...], sin_ref[...], pair_ref[...], height)
    value = v_ref[0].reshape(wide.shape)
    hi, lo = split_hi_lo(rot)
    outer = dot_t(hi, value) + dot_t(lo, value)
    lane = lax.broadcasted_iota(jnp.int32, (HD, LANES), 1)
    state = jnp.where(lane < HD, outer[:HD], outer[HD:])
    row = lax.broadcasted_iota(jnp.int32, (ROWS - HD, LANES), 0)
    total = jnp.broadcast_to(jnp.sum(wide, axis=0, keepdims=True), row.shape)
    joined = (blocks[0] == blocks[1]).astype(F32)
    marks = [blocks[g], frames[g], None, frames[1 - g]]
    extra = jnp.where(row == 0, total, 0.0)
    for i, mark in enumerate(marks):
        extra = jnp.where(row == i + 1, joined if mark is None else mark.astype(F32), extra)

    @pl.when(g == 0)
    def _():
        first_ref[:HD] = state
        first_ref[HD:] = extra

    @pl.when(g == 1)
    def _():
        second_ref[:HD] = state
        second_ref[HD:] = extra
        total_ref[:HD] = first_ref[:HD] + state
        total_ref[HD:] = first_ref[HD:] + extra
        lead_ref[:HD] = first_ref[:HD] + joined * state
        lead_ref[HD:] = first_ref[HD:] + jnp.where(row == 0, joined * extra, 0.0)


def query_kernel(q_ref, halo_ref, prev_ref, own_ref, freq_ref, cos_ref, sin_ref, pair_ref, _, qp_ref, hi_ref, lo_ref, __):
    e = pl.program_id(0)
    query = jnp.maximum(jnp.where(e < 2, halo_ref[0], q_ref[0]), 0)
    height, _, _ = query.shape
    here, other = HD + 2, HD + 4
    rows = [prev_ref[other : other + 1], prev_ref[here : here + 1], own_ref[other : other + 1], own_ref[here : here + 1]]
    position = jnp.where(e < 2, jnp.where(e == 0, rows[0], rows[1]), jnp.where(e == 2, rows[2], rows[3]))
    _, rot = rotated(query, freq_ref[...] * position, cos_ref[...], sin_ref[...], pair_ref[...], height)
    hi, lo = split_hi_lo(rot)
    qp_ref[...] = query.reshape(qp_ref.shape)
    hi_ref[...] = hi.reshape(hi_ref.shape)
    lo_ref[...] = lo.reshape(lo_ref.shape)


def finish_states(first, second, prev, upto, next_lead, far_lead, same_head, sh_ref, sl_ref, kh_ref, kl_ref):
    mark = slice(HD + 1, HD + 2)
    joint = slice(HD + 3, HD + 4)
    tail = jnp.where(next_lead[mark] == second[mark], next_lead, 0.0)
    tail = tail + jnp.where(far_lead[mark] == second[mark], far_lead, 0.0)
    state_1 = upto + first + second + tail
    state_0 = jnp.where(second[joint] > 0.5, state_1, upto + first)
    state_b = jnp.where(prev[mark] == first[mark], state_0, upto)
    state_a = jnp.where(prev[joint] > 0.5, state_b, upto - prev)
    lane = lax.broadcasted_iota(jnp.int32, (HD, LANES), 1)
    square = (LANES, LANES)
    eye = lax.broadcasted_iota(jnp.int32, square, 0) == lax.broadcasted_iota(jnp.int32, square, 1)
    for e, state in enumerate((state_a, state_b, state_0, state_1)):
        packed = state[:HD]
        full = jnp.concatenate([jnp.where(lane < HD, packed, 0.0), jnp.where(lane < HD, 0.0, packed)], axis=0)
        sh_ref[e], sl_ref[e] = split_hi_lo(full)
        d_hi, d_lo = split_hi_lo(jnp.where(eye, state[HD : HD + 1], 0.0))
        kh_ref[e], kl_ref[e] = split_hi_lo(dot(d_hi, same_head) + dot(d_lo, same_head))


def attend_kernel(
    flags, qp_ref, hi_ref, lo_ref, first_ref, second_ref, prev_ref, next_ref, far_ref, upto_ref, a_ref, b_ref, c_ref,
    same_ref, mine_ref, other_ref, rows_ref, sh_ref, sl_ref, kh_ref, kl_ref,
):
    height, frames, width, lanes = qp_ref.shape
    upto = upto_ref[...]
    for i, arrived in enumerate((a_ref, b_ref, c_ref)):
        upto = upto + jnp.where(flags[i + 1] != 0, arrived[...], 0.0)
    records = (first_ref[...], second_ref[...], prev_ref[...], upto, next_ref[...], far_ref[...])
    finish_states(*records, same_ref[...], sh_ref, sl_ref, kh_ref, kl_ref)
    mine = flags[0]
    for e in range(frames):
        query, hi, lo = (r[:, e].reshape(height * width, lanes) for r in (qp_ref, hi_ref, lo_ref))
        numerator = dot(hi, sh_ref[e]) + dot(lo, sh_ref[e]) + dot(hi, sl_ref[e])
        denominator = dot(query, kh_ref[e]) + dot(query, kl_ref[e]) + EPSILON
        rows_ref[...] = (numerator / denominator).astype(BF).reshape(height, width, lanes)
        for chip in range(height // 4):
            out = slice(2 * chip, 2 * chip + 2)
            mine_ref[out, e] = rows_ref[pl.ds(4 * chip + 2 * mine, 2)]
            other_ref[out, e] = rows_ref[pl.ds(4 * chip + 2 - 2 * mine, 2)]


def conv_kernel(count, idx, *refs):
    parts = (refs[:count], refs[count : 2 * count])
    weights = refs[2 * count : 2 * count + 2]
    outs = refs[2 * count + 2 :]
    width = parts[0][0].shape[2]
    each = 2 * width
    lhs = [
        [
            jnp.concatenate([b[:, 2 - tap + t].reshape(each, LANES) for b in blocks for t in range(2)], axis=0)
            for tap in range(3)
        ]
        for blocks in parts
    ]

    def columns(col, size):
        total = None
        for blocks, w_ref in zip(lhs, weights):
            for tap in range(3):
                part = dot(blocks[tap], w_ref[tap, :, col : col + size])
                total = part if total is None else total + part
        for j in range(count):
            for t in range(2):
                at = (2 * j + t) * each
                piece = total[at : at + each].reshape(2, width, size)
                for row in range(2):
                    out = outs[2 * j + row]
                    out[t, :, :size] = piece[row].astype(out.dtype)

    c_out = weights[0].shape[-1]
    for number, col in enumerate(range(0, c_out, TILE)):
        pl.when(pl.program_id(0) == number)(functools.partial(columns, col, min(TILE, c_out - col)))


TILE = 768
LIMIT = pltpu.CompilerParams(vmem_limit_bytes=24 << 20)


def off_chip(*values):
    return [pltpu.with_memory_space_constraint(v, pltpu.HBM) for v in values]


def whole(shape):
    return pl.BlockSpec(shape, lambda *_: (0,) * len(shape))


def attend(flags, queries, records, same_head):
    height, frames, width, lanes = queries[0].shape
    half = (height // 2, frames, width, lanes)
    square = pltpu.VMEM((frames, lanes, lanes), BF)
    in_vmem = pl.BlockSpec(memory_space=pltpu.VMEM)
    return pl.pallas_call(
        attend_kernel,
        grid_spec=pltpu.PrefetchScalarGridSpec(
            num_scalar_prefetch=1,
            grid=(1,),
            in_specs=[in_vmem] * 3 + [whole((ROWS, lanes))] * 9 + [whole((lanes, lanes))],
            out_specs=[in_vmem] * 2,
            scratch_shapes=[pltpu.VMEM((height, width, lanes), BF)] + [square] * 4,
        ),
        out_shape=[pltpu.VMEM(half, BF)] * 2,
        compiler_params=LIMIT,
        name="attend",
    )(flags, *queries, *records, same_head)


def add_kernel(a_ref, b_ref, c_ref, d_ref, first_ref, second_ref):
    first_ref[...] = (a_ref[...] + b_ref[...].astype(F32)).astype(BF)
    second_ref[...] = (c_ref[...] + d_ref[...].astype(F32)).astype(BF)


def final_kernel(*refs):
    bias_ref, out_ref = refs[-2:]
    for row in range(2):
        own, low, high = (r[...].astype(F32) for r in refs[3 * row : 3 * row + 3])
        total = own + low + high + bias_ref[...][None]
        out_ref[row] = (total / (1.0 + jnp.exp(-total))).astype(BF)


def conv_group(index, slots, attended, weights, dtypes):
    _, frames, width, lanes = attended[0].shape
    count = len(slots)
    c_out = weights[0].shape[-1]

    def row_block(slot):
        return pl.BlockSpec((2, frames, width, lanes), lambda n, idx: (idx[slot], 0, 0, 0))

    return pl.pallas_call(
        functools.partial(conv_kernel, count),
        grid_spec=pltpu.PrefetchScalarGridSpec(
            num_scalar_prefetch=1,
            grid=(pl.cdiv(c_out, TILE),),
            in_specs=[row_block(s) for _ in attended for s in slots] + [pl.BlockSpec(memory_space=pltpu.VMEM)] * 2,
            out_specs=[pl.BlockSpec((2, width, TILE), lambda n, idx: (0, 0, n))] * (2 * count),
        ),
        out_shape=[pltpu.HBM((2, width, c_out), dtype) for dtype in dtypes],
        compiler_params=LIMIT,
        name="conv",
    )(index, *[a for a in attended for _ in slots], *weights)


def shifted(value, by):
    length = lax.axis_size("frame")
    return lax.ppermute(value, "frame", [(i, i + by) for i in range(length) if 0 <= i + by < length])


def swapped(value, mask):
    return lax.ppermute(value, "frame", [(i, i ^ mask) for i in range(lax.axis_size("frame"))])


def moved(value, dy, dc):
    chips = lax.axis_size("head") // 2
    return lax.ppermute(
        value, "head", [(y * 2 + c, (y + dy) % chips * 2 + (c + dc) % 2) for y in range(chips) for c in range(2)]
    )


def block(
    queries, key_vectors, value_vectors, frame_index, height_index, width_index, frame_block, conv_weight, conv_bias
):
    frames, height, width, lanes = queries.shape
    c_out = conv_weight.shape[-1]
    pairing = jnp.asarray(PAIRING, BF)
    same_head = jnp.asarray(SAME_HEAD, BF)
    freq = jnp.asarray(FREQ)[None, :]
    frame_spec = pl.BlockSpec((1, height, width, lanes), lambda g, *_: (g, 0, 0, 0))
    record = (ROWS, lanes)
    table = (height + width, lanes)
    state_call = pl.pallas_call(
        state_kernel,
        grid_spec=pltpu.PrefetchScalarGridSpec(
            num_scalar_prefetch=4,
            grid=(frames,),
            in_specs=[frame_spec, frame_spec, whole((1, lanes)), whole((lanes, lanes))],
            out_specs=[whole(record)] * 4 + [whole(table)] * 2,
        ),
        out_shape=[pltpu.HBM(record, F32)] * 2
        + [jax.ShapeDtypeStruct(record, F32)] * 2
        + [pltpu.HBM(table, F32)] * 2,
        compiler_params=LIMIT,
        name="frame_state",
    )
    first, second, total, lead, side_cos, side_sin = state_call(*off_chip(frame_block, frame_index, height_index, width_index, key_vectors, value_vectors, freq, pairing))

    device = lax.axis_index("frame")
    depth = 8
    upto = jnp.zeros_like(total)
    running = total
    mask = 1
    while mask < depth:
        arrived = swapped(running, depth - 1 if 2 * mask == depth else mask)
        upto = upto + jnp.where(device & mask != 0, arrived, 0.0)
        running = running + arrived
        mask *= 2
    across = []
    while mask < lax.axis_size("frame"):
        across.append(swapped(running, mask))
        mask += depth

    their_weight = moved(conv_weight, 0, 1)
    halo = shifted(queries, 1)
    prev = shifted(second, 1)
    next_lead = shifted(lead, -1)
    sums = lax.broadcasted_iota(jnp.int32, (ROWS, 1), 0) <= HD
    mark = slice(HD + 1, HD + 2)
    chained = (next_lead[mark] == lead[mark]) & (lead[HD + 3 : HD + 4] > 0.5)
    pair_lead = lead + jnp.where(sums & chained, next_lead, 0.0)
    far_lead = shifted(pair_lead, -2)

    anywhere = pl.BlockSpec(memory_space=pl.ANY)
    query_block = pl.BlockSpec((height, 1, width, lanes), lambda e: (0, e, 0, 0))
    query_shape = pltpu.VMEM((height, 2 * frames, width, lanes), BF)
    query_call = pl.pallas_call(
        query_kernel,
        grid=(2 * frames,),
        in_specs=[
            pl.BlockSpec((1, height, width, lanes), lambda e: (jnp.maximum(e - 2, 0), 0, 0, 0)),
            pl.BlockSpec((1, height, width, lanes), lambda e: (jnp.minimum(e, 1), 0, 0, 0)),
            whole(record), whole(record), whole((1, lanes)), whole(table), whole(table), whole((lanes, lanes)), anywhere,
        ],
        out_specs=[query_block] * 3 + [anywhere],
        out_shape=[query_shape] * 3 + [pltpu.HBM(conv_weight.shape, BF)],
        input_output_aliases={8: 3},
        compiler_params=LIMIT,
        name="queries",
    )
    positive, rot_hi, rot_lo, their_weight = query_call(
        *off_chip(queries, halo, prev, second, freq, side_cos, side_sin, pairing, their_weight)
    )

    positive, rot_hi, rot_lo, across = lax.optimization_barrier((positive, rot_hi, rot_lo, across))
    records = (*off_chip(first, second, prev), next_lead, far_lead, upto, *across)

    head = lax.axis_index("head")
    chips = lax.axis_size("head") // 2
    chip, core = head // 2, head % 2
    (same,) = off_chip(same_head)
    owners = [(chip + j) % chips for j in (2, 1, 3, 0)]
    flags = jnp.stack([core] + [(device ^ m < device).astype(jnp.int32) for m in (8, 16, 24)] + owners).astype(jnp.int32)
    mine, other = attend(flags, (positive, rot_hi, rot_lo), records, same)
    theirs = moved(other, 0, 1)
    attended = (mine, theirs)
    weights = [pltpu.with_memory_space_constraint(w, pltpu.VMEM) for w in (conv_weight, their_weight)]
    far = conv_group(flags, (4,), attended, weights, (BF, BF))
    up = moved(far[0], 1, 0)
    down = moved(far[1], 3, 0)
    near = conv_group(flags, (5, 6), attended, weights, (F32, BF, BF, F32))
    low_1 = moved(near[1], 1, 0)
    high_0 = moved(near[2], 3, 0)
    row = (frames, width, c_out)
    in_vmem = pl.BlockSpec(memory_space=pltpu.VMEM)
    joined_low, joined_high = pl.pallas_call(
        add_kernel,
        in_specs=[whole(row), in_vmem, whole(row), in_vmem],
        out_specs=[whole(row)] * 2,
        out_shape=[pltpu.HBM(row, BF)] * 2,
        compiler_params=LIMIT,
        name="join",
    )(*off_chip(near[0]), up, *off_chip(near[3]), down)
    low_0 = moved(joined_low, 1, 0)
    high_1 = moved(joined_high, 3, 0)
    own = conv_group(flags, (7,), attended, weights, (F32, F32))
    return pl.pallas_call(
        final_kernel,
        in_specs=[whole(row), in_vmem, in_vmem] * 2 + [whole((1, c_out))],
        out_specs=whole((2, *row)),
        out_shape=jax.ShapeDtypeStruct((2, *row), BF),
        compiler_params=LIMIT,
        name="silu",
    )(*off_chip(own[0]), low_0, high_0, *off_chip(own[1]), low_1, high_1, conv_bias[None])


def solution(mesh):
    placed = (
        P("frame", None, None, "head"),
        P("frame", None, None, "head"),
        P("frame", None, None, "head"),
        P("frame"),
        P(),
        P(),
        P("frame"),
        P(None, "head", None),
        P(),
    )
    return jax.shard_map(
        block,
        mesh=mesh,
        in_specs=placed,
        out_specs=P("head", "frame", None, None),
        check_vma=False,
    )
```

```python
import functools

import jax
import jax.numpy as jnp
import numpy as np
from jax import lax
from jax.experimental import pallas as pl
from jax.experimental.pallas import tpu as pltpu
from jax.sharding import PartitionSpec as P


HD = 112
LANES = 2 * HD
SIDE = HD * 5 // 14 // 2 * 2
ROWS = 120
EPSILON = 1e-06
BF = jnp.bfloat16
F32 = jnp.float32


def lane_tables():
    first = HD - 2 * SIDE
    freq = np.zeros(LANES, np.float64)
    section = np.zeros(LANES, np.int32)
    pairing = np.zeros((LANES, LANES), np.float32)
    for head in range(2):
        start = head * HD
        for number, size in enumerate((first, SIDE, SIDE)):
            half = size // 2
            for j in range(half):
                low, high = start + j, start + j + half
                freq[low] = freq[high] = 10000.0 ** (-2.0 * j / size)
                section[low] = section[high] = number
                pairing[high, low] = -1.0
                pairing[low, high] = 1.0
            start += size
    same_head = (np.arange(LANES)[:, None] // HD == np.arange(LANES)[None, :] // HD).astype(np.float32)
    return freq.astype(np.float32), section, pairing, same_head


FREQ, _, PAIRING, SAME_HEAD = lane_tables()


def split_hi_lo(value):
    hi = value.astype(BF)
    return hi, (value - hi.astype(F32)).astype(BF)


def dot(a, b):
    return jnp.dot(a, b, preferred_element_type=F32)


def dot_t(a, b):
    return lax.dot_general(a, b, (((0,), (0,)), ((), ())), preferred_element_type=F32)


def side_angles(heights, widths, freq, cos_ref, sin_ref):
    rows, cols = heights.shape[0], widths.shape[0]
    positions = [heights[i] for i in range(rows)] + [widths[i] for i in range(cols)]
    lane = lax.broadcasted_iota(jnp.int32, (rows + cols, LANES), 1)
    lane = jnp.where(lane < HD, lane, lane - HD)
    row = lax.broadcasted_iota(jnp.int32, lane.shape, 0)
    first = HD - 2 * SIDE
    section = (lane >= first).astype(jnp.int32) + (lane >= first + SIDE).astype(jnp.int32)
    mine = section == jnp.where(row < rows, 1, 2)
    for i, position in enumerate(positions):
        cos_ref[i : i + 1] = freq * position.astype(F32)
    angles = cos_ref[...]
    sin_ref[...] = jnp.where(mine, jnp.sin(angles), 0.0)
    cos_ref[...] = jnp.where(mine, jnp.cos(angles), 0.0)


def time_tables(angle):
    lane = lax.broadcasted_iota(jnp.int32, angle.shape, 1)
    mine = jnp.where(lane < HD, lane, lane - HD) < HD - 2 * SIDE
    return jnp.where(mine, jnp.cos(angle), 0.0), jnp.where(mine, jnp.sin(angle), 0.0)


def rotated(positive, angle, side_cos, side_sin, pairing, height):
    _, width, lanes = positive.shape
    flat = positive.reshape(height * width, lanes)
    partner = dot(flat, pairing)
    time_cos, time_sin = time_tables(angle)
    cos = (side_cos[:height] + time_cos)[:, None, :] + side_cos[height:][None, :, :]
    sin = (side_sin[:height] + time_sin)[:, None, :] + side_sin[height:][None, :, :]
    wide = flat.astype(F32)
    return wide, wide * cos.reshape(height * width, lanes) + partner * sin.reshape(height * width, lanes)


def state_kernel(
    blocks, frames, heights, widths, k_ref, v_ref, freq_ref, pair_ref,
    first_ref, second_ref, total_ref, lead_ref, cos_ref, sin_ref,
):
    g = pl.program_id(0)
    height = k_ref.shape[1]

    @pl.when(g == 0)
    def _():
        side_angles(heights, widths, freq_ref[...], cos_ref, sin_ref)

    key = jnp.maximum(k_ref[0], 0)
    angle = freq_ref[...] * frames[g].astype(F32)
    wide, rot = rotated(key, angle, cos_ref[...], sin_ref[...], pair_ref[...], height)
    value = v_ref[0].reshape(wide.shape)
    hi, lo = split_hi_lo(rot)
    outer = dot_t(hi, value) + dot_t(lo, value)
    lane = lax.broadcasted_iota(jnp.int32, (HD, LANES), 1)
    state = jnp.where(lane < HD, outer[:HD], outer[HD:])
    row = lax.broadcasted_iota(jnp.int32, (ROWS - HD, LANES), 0)
    total = jnp.broadcast_to(jnp.sum(wide, axis=0, keepdims=True), row.shape)
    joined = (blocks[0] == blocks[1]).astype(F32)
    marks = [blocks[g], frames[g], None, frames[1 - g]]
    extra = jnp.where(row == 0, total, 0.0)
    for i, mark in enumerate(marks):
        extra = jnp.where(row == i + 1, joined if mark is None else mark.astype(F32), extra)

    @pl.when(g == 0)
    def _():
        first_ref[:HD] = state
        first_ref[HD:] = extra

    @pl.when(g == 1)
    def _():
        second_ref[:HD] = state
        second_ref[HD:] = extra
        total_ref[:HD] = first_ref[:HD] + state
        total_ref[HD:] = first_ref[HD:] + extra
        lead_ref[:HD] = first_ref[:HD] + joined * state
        lead_ref[HD:] = first_ref[HD:] + jnp.where(row == 0, joined * extra, 0.0)


def query_kernel(q_ref, halo_ref, prev_ref, own_ref, freq_ref, cos_ref, sin_ref, pair_ref, _, qp_ref, hi_ref, lo_ref, __):
    e = pl.program_id(0)
    query = jnp.maximum(jnp.where(e < 2, halo_ref[0], q_ref[0]), 0)
    height, _, _ = query.shape
    here, other = HD + 2, HD + 4
    rows = [prev_ref[other : other + 1], prev_ref[here : here + 1], own_ref[other : other + 1], own_ref[here : here + 1]]
    position = jnp.where(e < 2, jnp.where(e == 0, rows[0], rows[1]), jnp.where(e == 2, rows[2], rows[3]))
    _, rot = rotated(query, freq_ref[...] * position, cos_ref[...], sin_ref[...], pair_ref[...], height)
    hi, lo = split_hi_lo(rot)
    qp_ref[...] = query.reshape(qp_ref.shape)
    hi_ref[...] = hi.reshape(hi_ref.shape)
    lo_ref[...] = lo.reshape(lo_ref.shape)


def finish_states(first, second, prev, upto, next_lead, far_lead, same_head, sh_ref, sl_ref, kh_ref, kl_ref):
    mark = slice(HD + 1, HD + 2)
    joint = slice(HD + 3, HD + 4)
    tail = jnp.where(next_lead[mark] == second[mark], next_lead, 0.0)
    tail = tail + jnp.where(far_lead[mark] == second[mark], far_lead, 0.0)
    state_1 = upto + first + second + tail
    state_0 = jnp.where(second[joint] > 0.5, state_1, upto + first)
    state_b = jnp.where(prev[mark] == first[mark], state_0, upto)
    state_a = jnp.where(prev[joint] > 0.5, state_b, upto - prev)
    lane = lax.broadcasted_iota(jnp.int32, (HD, LANES), 1)
    square = (LANES, LANES)
    eye = lax.broadcasted_iota(jnp.int32, square, 0) == lax.broadcasted_iota(jnp.int32, square, 1)
    for e, state in enumerate((state_a, state_b, state_0, state_1)):
        packed = state[:HD]
        full = jnp.concatenate([jnp.where(lane < HD, packed, 0.0), jnp.where(lane < HD, 0.0, packed)], axis=0)
        sh_ref[e], sl_ref[e] = split_hi_lo(full)
        d_hi, d_lo = split_hi_lo(jnp.where(eye, state[HD : HD + 1], 0.0))
        kh_ref[e], kl_ref[e] = split_hi_lo(dot(d_hi, same_head) + dot(d_lo, same_head))


def attend_kernel(
    flags, qp_ref, hi_ref, lo_ref, first_ref, second_ref, prev_ref, next_ref, far_ref, upto_ref, a_ref, b_ref, c_ref,
    same_ref, mine_ref, other_ref, rows_ref, sh_ref, sl_ref, kh_ref, kl_ref,
):
    height, frames, width, lanes = qp_ref.shape
    upto = upto_ref[...]
    for i, arrived in enumerate((a_ref, b_ref, c_ref)):
        upto = upto + jnp.where(flags[i + 1] != 0, arrived[...], 0.0)
    records = (first_ref[...], second_ref[...], prev_ref[...], upto, next_ref[...], far_ref[...])
    finish_states(*records, same_ref[...], sh_ref, sl_ref, kh_ref, kl_ref)
    mine = flags[0]
    for e in range(frames):
        query, hi, lo = (r[:, e].reshape(height * width, lanes) for r in (qp_ref, hi_ref, lo_ref))
        numerator = dot(hi, sh_ref[e]) + dot(lo, sh_ref[e]) + dot(hi, sl_ref[e])
        denominator = dot(query, kh_ref[e]) + dot(query, kl_ref[e]) + EPSILON
        rows_ref[...] = (numerator / denominator).astype(BF).reshape(height, width, lanes)
        for chip in range(height // 4):
            out = slice(2 * chip, 2 * chip + 2)
            mine_ref[out, e] = rows_ref[pl.ds(4 * chip + 2 * mine, 2)]
            other_ref[out, e] = rows_ref[pl.ds(4 * chip + 2 - 2 * mine, 2)]


def conv_kernel(count, idx, *refs):
    parts = (refs[:count], refs[count : 2 * count])
    weights = refs[2 * count : 2 * count + 2]
    outs = refs[2 * count + 2 :]
    width = parts[0][0].shape[2]
    each = 2 * width
    lhs = [
        [
            jnp.concatenate([b[:, 2 - tap + t].reshape(each, LANES) for b in blocks for t in range(2)], axis=0)
            for tap in range(3)
        ]
        for blocks in parts
    ]

    def columns(col, size):
        total = None
        for blocks, w_ref in zip(lhs, weights):
            for tap in range(3):
                part = dot(blocks[tap], w_ref[tap, :, col : col + size])
                total = part if total is None else total + part
        for j in range(count):
            for t in range(2):
                at = (2 * j + t) * each
                piece = total[at : at + each].reshape(2, width, size)
                for row in range(2):
                    out = outs[2 * j + row]
                    out[t, :, col : col + size] = piece[row].astype(out.dtype)

    c_out = weights[0].shape[-1]
    for number, col in enumerate(range(0, c_out, TILE)):
        pl.when(pl.program_id(0) == number)(functools.partial(columns, col, min(TILE, c_out - col)))


TILE = 768
LIMIT = pltpu.CompilerParams(vmem_limit_bytes=24 << 20)


def off_chip(*values):
    return [pltpu.with_memory_space_constraint(v, pltpu.HBM) for v in values]


def whole(shape):
    return pl.BlockSpec(shape, lambda *_: (0,) * len(shape))


def attend(flags, queries, records, same_head):
    height, frames, width, lanes = queries[0].shape
    half = (height // 2, frames, width, lanes)
    square = pltpu.VMEM((frames, lanes, lanes), BF)
    in_vmem = pl.BlockSpec(memory_space=pltpu.VMEM)
    return pl.pallas_call(
        attend_kernel,
        grid_spec=pltpu.PrefetchScalarGridSpec(
            num_scalar_prefetch=1,
            grid=(1,),
            in_specs=[in_vmem] * 3 + [whole((ROWS, lanes))] * 9 + [whole((lanes, lanes))],
            out_specs=[in_vmem] * 2,
            scratch_shapes=[pltpu.VMEM((height, width, lanes), BF)] + [square] * 4,
        ),
        out_shape=[pltpu.VMEM(half, BF)] * 2,
        compiler_params=LIMIT,
        name="attend",
    )(flags, *queries, *records, same_head)


def add_kernel(a_ref, b_ref, c_ref, d_ref, first_ref, second_ref):
    first_ref[...] = (a_ref[...] + b_ref[...].astype(F32)).astype(BF)
    second_ref[...] = (c_ref[...] + d_ref[...].astype(F32)).astype(BF)


def final_kernel(*refs):
    bias_ref, out_ref = refs[-2:]
    for row in range(2):
        own, low, high = (r[...].astype(F32) for r in refs[3 * row : 3 * row + 3])
        total = own + low + high + bias_ref[...][None]
        out_ref[row] = (total / (1.0 + jnp.exp(-total))).astype(BF)


def conv_group(index, slots, attended, weights, dtypes):
    _, frames, width, lanes = attended[0].shape
    count = len(slots)
    c_out = weights[0].shape[-1]

    def row_block(slot):
        return pl.BlockSpec((2, frames, width, lanes), lambda n, idx: (idx[slot], 0, 0, 0))

    return pl.pallas_call(
        functools.partial(conv_kernel, count),
        grid_spec=pltpu.PrefetchScalarGridSpec(
            num_scalar_prefetch=1,
            grid=(pl.cdiv(c_out, TILE),),
            in_specs=[row_block(s) for _ in attended for s in slots] + [pl.BlockSpec(memory_space=pltpu.VMEM)] * 2,
            out_specs=[pl.BlockSpec(memory_space=pltpu.VMEM)] * (2 * count),
        ),
        out_shape=[pltpu.VMEM((2, width, c_out), dtype) for dtype in dtypes],
        compiler_params=LIMIT,
        name="conv",
    )(index, *[a for a in attended for _ in slots], *weights)


def shifted(value, by):
    length = lax.axis_size("frame")
    return lax.ppermute(value, "frame", [(i, i + by) for i in range(length) if 0 <= i + by < length])


def swapped(value, mask):
    return lax.ppermute(value, "frame", [(i, i ^ mask) for i in range(lax.axis_size("frame"))])


def moved(value, dy, dc):
    chips = lax.axis_size("head") // 2
    return lax.ppermute(
        value, "head", [(y * 2 + c, (y + dy) % chips * 2 + (c + dc) % 2) for y in range(chips) for c in range(2)]
    )


def block(
    queries, key_vectors, value_vectors, frame_index, height_index, width_index, frame_block, conv_weight, conv_bias
):
    frames, height, width, lanes = queries.shape
    c_out = conv_weight.shape[-1]
    pairing = jnp.asarray(PAIRING, BF)
    same_head = jnp.asarray(SAME_HEAD, BF)
    freq = jnp.asarray(FREQ)[None, :]
    frame_spec = pl.BlockSpec((1, height, width, lanes), lambda g, *_: (g, 0, 0, 0))
    record = (ROWS, lanes)
    table = (height + width, lanes)
    state_call = pl.pallas_call(
        state_kernel,
        grid_spec=pltpu.PrefetchScalarGridSpec(
            num_scalar_prefetch=4,
            grid=(frames,),
            in_specs=[frame_spec, frame_spec, whole((1, lanes)), whole((lanes, lanes))],
            out_specs=[whole(record)] * 4 + [whole(table)] * 2,
        ),
        out_shape=[pltpu.HBM(record, F32)] * 2
        + [jax.ShapeDtypeStruct(record, F32)] * 2
        + [pltpu.HBM(table, F32)] * 2,
        compiler_params=LIMIT,
        name="frame_state",
    )
    first, second, total, lead, side_cos, side_sin = state_call(*off_chip(frame_block, frame_index, height_index, width_index, key_vectors, value_vectors, freq, pairing))

    device = lax.axis_index("frame")
    depth = 8
    upto = jnp.zeros_like(total)
    running = total
    mask = 1
    while mask < depth:
        arrived = swapped(running, depth - 1 if 2 * mask == depth else mask)
        upto = upto + jnp.where(device & mask != 0, arrived, 0.0)
        running = running + arrived
        mask *= 2
    across = []
    while mask < lax.axis_size("frame"):
        across.append(swapped(running, mask))
        mask += depth

    their_weight = moved(conv_weight, 0, 1)
    halo = shifted(queries, 1)
    prev = shifted(second, 1)
    next_lead = shifted(lead, -1)
    sums = lax.broadcasted_iota(jnp.int32, (ROWS, 1), 0) <= HD
    mark = slice(HD + 1, HD + 2)
    chained = (next_lead[mark] == lead[mark]) & (lead[HD + 3 : HD + 4] > 0.5)
    pair_lead = lead + jnp.where(sums & chained, next_lead, 0.0)
    far_lead = shifted(pair_lead, -2)

    anywhere = pl.BlockSpec(memory_space=pl.ANY)
    query_block = pl.BlockSpec((height, 1, width, lanes), lambda e: (0, e, 0, 0))
    query_shape = pltpu.VMEM((height, 2 * frames, width, lanes), BF)
    query_call = pl.pallas_call(
        query_kernel,
        grid=(2 * frames,),
        in_specs=[
            pl.BlockSpec((1, height, width, lanes), lambda e: (jnp.maximum(e - 2, 0), 0, 0, 0)),
            pl.BlockSpec((1, height, width, lanes), lambda e: (jnp.minimum(e, 1), 0, 0, 0)),
            whole(record), whole(record), whole((1, lanes)), whole(table), whole(table), whole((lanes, lanes)), anywhere,
        ],
        out_specs=[query_block] * 3 + [anywhere],
        out_shape=[query_shape] * 3 + [pltpu.HBM(conv_weight.shape, BF)],
        input_output_aliases={8: 3},
        compiler_params=LIMIT,
        name="queries",
    )
    positive, rot_hi, rot_lo, their_weight = query_call(
        *off_chip(queries, halo, prev, second, freq, side_cos, side_sin, pairing, their_weight)
    )

    positive, rot_hi, rot_lo, across = lax.optimization_barrier((positive, rot_hi, rot_lo, across))
    records = (*off_chip(first, second, prev), next_lead, far_lead, upto, *across)

    head = lax.axis_index("head")
    chips = lax.axis_size("head") // 2
    chip, core = head // 2, head % 2
    (same,) = off_chip(same_head)
    owners = [(chip + j) % chips for j in (2, 1, 3, 0)]
    flags = jnp.stack([core] + [(device ^ m < device).astype(jnp.int32) for m in (8, 16, 24)] + owners).astype(jnp.int32)
    mine, other = attend(flags, (positive, rot_hi, rot_lo), records, same)
    theirs = moved(other, 0, 1)
    attended = (mine, theirs)
    weights = [pltpu.with_memory_space_constraint(w, pltpu.VMEM) for w in (conv_weight, their_weight)]
    far = conv_group(flags, (4,), attended, weights, (BF, BF))
    up = moved(far[0], 1, 0)
    down = moved(far[1], 3, 0)
    near = conv_group(flags, (5, 6), attended, weights, (F32, BF, BF, F32))
    low_1 = moved(near[1], 1, 0)
    high_0 = moved(near[2], 3, 0)
    row = (frames, width, c_out)
    in_vmem = pl.BlockSpec(memory_space=pltpu.VMEM)
    joined_low, joined_high = pl.pallas_call(
        add_kernel,
        in_specs=[in_vmem] * 4,
        out_specs=[in_vmem] * 2,
        out_shape=[pltpu.VMEM(row, BF)] * 2,
        compiler_params=LIMIT,
        name="join",
    )(near[0], up, near[3], down)
    low_0 = moved(joined_low, 1, 0)
    high_1 = moved(joined_high, 3, 0)
    own = conv_group(flags, (7,), attended, weights, (F32, F32))
    return pl.pallas_call(
        final_kernel,
        in_specs=[in_vmem] * 6 + [whole((1, c_out))],
        out_specs=whole((2, *row)),
        out_shape=jax.ShapeDtypeStruct((2, *row), BF),
        compiler_params=LIMIT,
        name="silu",
    )(own[0], low_0, high_0, own[1], low_1, high_1, conv_bias[None])


def solution(mesh):
    placed = (
        P("frame", None, None, "head"),
        P("frame", None, None, "head"),
        P("frame", None, None, "head"),
        P("frame"),
        P(),
        P(),
        P("frame"),
        P(None, "head", None),
        P(),
    )
    return jax.shard_map(
        block,
        mesh=mesh,
        in_specs=placed,
        out_specs=P("head", "frame", None, None),
        check_vma=False,
    )
```
